256 devices in a mesh: frames: 32 (over z, y), heads: 8 (over x, core).
Axes of the slice: x: 4, y: 4, z: 8, core: 2. Of those that a mesh axis runs over, the one named last changes fastest.
Arguments:
- bank_query: bfloat16 [64, 256, 5120], P(None, 'frames', 'heads'), may hold values from -2048 to 2048
- char_bank: bfloat16 [2, 8, 768, 5120], P(None, None, 'frames', 'heads'), may hold values from -8 to 8
- char_slots: int32 [32, 2], replicated, may hold values from 0 to 7, as said below
- slot_live: int32 [32, 2], replicated, may hold values from 0 to 1, as said below
- frame_tokens: bfloat16 [3, 64, 256, 5120], P(None, None, 'frames', 'heads'), may hold values from -2048 to 2048
- out_weight: bfloat16 [5120, 5120], P('heads'), may hold values from -0.078125 to 0.078125
Outputs:
- blended: bfloat16 [64, 256, 5120], P('heads', 'frames')
The draws below stay inside these ranges and needn't reach their ends.
Inputs may be any that keep to these rules, and one draw needn't show every extreme that they name: `char_slots`: the two ids of a shard differ. `slot_live`: slot 0 of every shard is 1.
All inputs are finite; a program needn't handle non-finite values.
Results may differ from the reference program's by a relative error of at most 0.014.
Values may be sent and summed in bfloat16 or wider, within the bound.
A program may use at most 128 MiB of HBM per device.

```python
import jax
import jax.numpy as jnp
from jax import lax

D = 5120
HEADS = 40
HEAD_DIM = 128
CHARACTERS = 8
REF_TOKENS = 768
FRAMES_DEV = 8
SPATIAL = 64
FRAMES = 256
SHARDS = 32
GROUP_WIDTH = 640
N_HEADS = 8


def pick_chars(key):
    base_key = jax.random.fold_in(key, 101)
    key_first, key_offset = jax.random.split(base_key)
    first_char = jax.random.randint(key_first, (SHARDS,), 0, CHARACTERS)
    offset = jax.random.randint(key_offset, (SHARDS,), 1, CHARACTERS)
    second = (first_char + offset) % CHARACTERS
    return jnp.stack([first_char, second], axis=1).astype(jnp.int32)


def make_bank(key):
    base_key = jax.random.fold_in(key, 103)
    key_keys, key_values = jax.random.split(base_key)
    key_rows = jnp.clip(jax.random.normal(key_keys, (CHARACTERS, REF_TOKENS, D), jnp.float32), -5.0, 5.0) * 1.6
    value_rows = jnp.clip(jax.random.normal(key_values, (CHARACTERS, REF_TOKENS, D), jnp.float32), -5.0, 5.0)
    return jnp.stack([key_rows, value_rows])


def draw_char_slots(key, part):
    return pick_chars(key)


def draw_slot_live(key, part):
    second = jax.random.randint(jax.random.fold_in(key, 102), (SHARDS,), 0, 2)
    return jnp.stack([jnp.ones_like(second), second], axis=1).astype(jnp.int32)


def draw_char_bank(key, part):
    return make_bank(key).astype(jnp.bfloat16)


def draw_bank_query(key, part):
    queries = jnp.clip(jax.random.normal(jax.random.fold_in(key, 104), (SPATIAL, FRAMES, D), jnp.float32), -5.0, 5.0) * 1.6
    return queries.astype(jnp.bfloat16)


def draw_frame_tokens(key, part):
    raw = jnp.clip(jax.random.normal(jax.random.fold_in(key, 105), (3, SPATIAL, FRAMES, D), jnp.float32), -5.0, 5.0)
    raw = raw * jnp.array([1.4, 1.4, 1.0], jnp.float32)[:, None, None, None]
    return raw.astype(jnp.bfloat16)


def block_scale(stream_key, shape, cuts, smallest, high):
    def one(position, parts):
        draws = jax.random.uniform(jax.random.fold_in(jax.random.fold_in(stream_key, 6), position), (parts,), jnp.float32, smallest / len(cuts), high / len(cuts))
        return jnp.repeat(jnp.exp(draws), shape[position] // parts).reshape((-1,) + (1,) * (len(shape) - position - 1))

    loudness = one(*cuts[0])
    for cut in cuts[1:]:
        loudness = loudness * one(*cut)
    return loudness


def bell_draw(key, dims, deviation, bound, cuts=(), held_as=jnp.bfloat16):
    values = deviation * jax.random.normal(key, dims, jnp.float32)
    if cuts:
        values = values * block_scale(key, dims, cuts, -0.22, 0.18)
    return jnp.clip(values, -bound, bound).astype(held_as)


def setup_inputs(seed: int = 0) -> dict:
    key_of = jax.random.split(jax.random.key(seed), 7)
    return {
        "bank_query": draw_bank_query(jax.random.fold_in(key_of[6], 71), 0),
        "char_bank": draw_char_bank(jax.random.fold_in(key_of[6], 71), 0),
        "char_slots": draw_char_slots(jax.random.fold_in(key_of[6], 71), 0),
        "slot_live": draw_slot_live(jax.random.fold_in(key_of[6], 71), 0),
        "frame_tokens": draw_frame_tokens(jax.random.fold_in(key_of[6], 71), 0),
        "out_weight": bell_draw(key_of[5], (D, D), D ** -0.5, 0.078125, ((0, 8),)),
    }


def bank_attend(operands, char_bank):
    queries, listed, opened = operands
    key_rows = char_bank[0][listed].reshape(2 * REF_TOKENS, HEADS, HEAD_DIM)
    value_rows = char_bank[1][listed].reshape(2 * REF_TOKENS, HEADS, HEAD_DIM)
    live_rows = jnp.repeat(opened > 0, REF_TOKENS)
    scores = jnp.einsum("sfhd,khd->sfhk", queries.astype(jnp.float32), key_rows.astype(jnp.float32)) * (HEAD_DIM ** -0.5)
    masked = jnp.where(live_rows, scores, -jnp.inf)
    peak = jnp.max(masked, axis=-1, keepdims=True)
    weights = jnp.exp(masked - peak)
    totals = jnp.sum(weights, axis=-1, keepdims=True)
    rounded = lax.optimization_barrier(weights.astype(jnp.bfloat16)).astype(jnp.float32)
    attended = jnp.einsum("sfhk,khd->sfhd", rounded, value_rows.astype(jnp.float32))
    return attended / totals


def frame_attend(tokens):
    queries = tokens[0].astype(jnp.float32)
    key_rows = tokens[1].astype(jnp.float32)
    value_rows = tokens[2].astype(jnp.float32)
    scores = jnp.einsum("fhd,ghd->fhg", queries, key_rows) * (HEAD_DIM ** -0.5)
    peak = jnp.max(scores, axis=-1, keepdims=True)
    weights = jnp.exp(scores - peak)
    totals = jnp.sum(weights, axis=-1, keepdims=True)
    rounded = lax.optimization_barrier(weights.astype(jnp.bfloat16)).astype(jnp.float32)
    attended = jnp.einsum("fhg,ghd->fhd", rounded, value_rows) / totals
    return attended.astype(jnp.bfloat16)


def reference(bank_query, char_bank, char_slots, slot_live, frame_tokens, out_weight):
    grouped = bank_query.reshape(SPATIAL, SHARDS, FRAMES_DEV, HEADS, HEAD_DIM)
    grouped = jnp.moveaxis(grouped, 1, 0)
    ref_out = lax.map(lambda operands: bank_attend(operands, char_bank), (grouped, char_slots, slot_live))
    ref_out = jnp.moveaxis(ref_out, 0, 1).reshape(SPATIAL, FRAMES, D)
    tokens = jnp.moveaxis(frame_tokens.reshape(3, SPATIAL, FRAMES, HEADS, HEAD_DIM), 1, 0)
    frame_out = lax.map(frame_attend, tokens).reshape(SPATIAL, FRAMES, D)
    combined = (ref_out + frame_out.astype(jnp.float32)).astype(jnp.bfloat16).reshape(SPATIAL * FRAMES, D)
    summed = jnp.zeros((SPATIAL * FRAMES, D), jnp.float32)
    for group in range(N_HEADS):
        low = group * GROUP_WIDTH
        partial_sum = jnp.dot(combined[:, low:low + GROUP_WIDTH], out_weight[low:low + GROUP_WIDTH], preferred_element_type=jnp.float32)
        summed = summed + lax.optimization_barrier(partial_sum.astype(jnp.bfloat16)).astype(jnp.float32)
    return summed.astype(jnp.bfloat16).reshape(SPATIAL, FRAMES, D)
```

```python
import functools

import jax
import jax.numpy as jnp
from jax import lax
from jax.experimental import pallas as pl
from jax.experimental.pallas import tpu as pltpu
from jax.sharding import PartitionSpec as P

HEAD_DIM = 128
ROWS_Y = 4
EXP2_SCALE = HEAD_DIM ** -0.5 * 1.4426950408889634
FAR = 1e30
MESH = pl.DeviceIdType.MESH


def dot_t(a, b):
    return lax.dot_general(a, b, (((1,), (1,)), ((), ())), preferred_element_type=jnp.float32)


def dot(a, b):
    return jnp.dot(a, b, preferred_element_type=jnp.float32)


def await_bytes(ref, sem):
    pltpu.make_async_copy(ref, ref, sem).wait()


def kernel(dims, slots, live, queries, bank, tokens, weight, out, *scratch):
    shards, levels, chips = dims
    held = (scratch[0:levels], scratch[levels:2 * levels])
    (picked, listed, qv, wv, qkv, o_here, o_back, ref_out, combined, part, pair, summed, from_left_half,
     from_right_half, from_left, from_right, local_sem, ring_send, ring_recv, pick_send, pick_recv, token_send,
     token_recv, o_send, o_recv, pair_send, pair_recv, sum_send, sum_recv, own_sem) = scratch[2 * levels:]
    spatial, here, width = queries.shape
    heads = width // HEAD_DIM
    mine = spatial // shards
    f = lax.axis_index("frames")
    r = lax.axis_index("heads")
    z, y = lax.div(f, ROWS_Y), lax.rem(f, ROWS_Y)
    x, core = lax.div(r, 2), lax.rem(r, 2)
    up = lax.rem(z + 1, levels) * ROWS_Y + y
    down = lax.rem(z + levels - 1, levels) * ROWS_Y + y
    twin = r + 1 - 2 * core
    right = lax.rem(x + 1, chips) * 2 + core
    left = lax.rem(x + chips - 1, chips) * 2 + core

    def peer(i):
        k, dy = lax.div(i, ROWS_Y), lax.rem(i, ROWS_Y)
        odd = lax.rem(k, 2)
        dz = odd * lax.div(k + 1, 2) + (1 - odd) * (levels - lax.div(k, 2))
        return lax.rem(z + dz, levels) * ROWS_Y + lax.rem(y + dy, ROWS_Y)

    def remote(src, dst, send, recv, **where):
        copy = pltpu.make_async_remote_copy(
            src_ref=src, dst_ref=dst, send_sem=send, recv_sem=recv, device_id=where, device_id_type=MESH
        )
        copy.start()
        return copy

    own = [pltpu.make_async_copy(bank.at[kv], held[kv][0], local_sem.at[kv]) for kv in range(2)]
    load_q = pltpu.make_async_copy(queries, qv, local_sem.at[2])
    load_w = pltpu.make_async_copy(weight, wv, local_sem.at[3])
    keep = pltpu.make_async_copy(tokens.at[:, pl.ds(mine * f, mine)], qkv.at[:, :, f], local_sem.at[4])
    for copy in (*own, load_q, keep, load_w):
        copy.start()

    barrier = pltpu.get_barrier_semaphore()

    @pl.loop(1, shards)
    def _(i):
        pl.semaphore_signal(barrier, inc=1, device_id={"frames": peer(i)}, device_id_type=MESH)

    for near in (twin, right, left):
        pl.semaphore_signal(barrier, inc=1, device_id={"heads": near}, device_id_type=MESH)
    pl.semaphore_wait(barrier, shards - 1 + 3)

    half = levels // 2
    sends = []

    def pass_on(kv, src, rel, upward):
        ref = bank.at[kv] if src == 0 else held[kv][src]
        sends.append(
            remote(ref, held[kv][rel], ring_send.at[kv, rel], ring_recv.at[kv, rel], frames=up if upward else down)
        )

    def pick(kv, rel):
        for dy in range(ROWS_Y):
            shard = z * ROWS_Y + lax.rem(y + dy, ROWS_Y)
            for j in range(2):
                block = held[kv][rel][slots[shard, j]]
                if dy:
                    picked[kv, rel, dy - 1, j] = block
                else:
                    listed[kv, j, rel, 0] = block
        for dy in range(1, ROWS_Y):
            remote(
                picked.at[kv, rel, dy - 1], listed.at[kv, :, rel, dy], pick_send, pick_recv.at[kv],
                frames=z * ROWS_Y + lax.rem(y + dy, ROWS_Y),
            )

    for kv in range(2):
        pass_on(kv, 0, 1, True)
        pass_on(kv, 0, levels - 1, False)
    for kv in range(2):
        own[kv].wait()
        pick(kv, 0)

    def send_tokens():
        @pl.loop(1, shards)
        def _(i):
            p = peer(i)
            remote(tokens.at[:, pl.ds(mine * p, mine)], qkv.at[:, :, f], token_send, token_recv, frames=p)

    for step in range(1, half + 1):
        for kv in range(2):
            for rel, upward in ((step, True), (levels - step, False)):
                if step == half and upward != (kv == 0):
                    continue
                await_bytes(held[kv][rel], ring_recv.at[kv, rel])
                last = half if upward == (kv == 0) else half - 1
                if step < last:
                    pass_on(kv, rel, rel + 1 if upward else rel - 1, upward)
                if step < half:
                    pick(kv, rel)
        if step == half - 1:
            send_tokens()
    for kv in range(2):
        pick(kv, half)

    load_q.wait()
    for kv in range(2):
        await_bytes(listed.at[kv, :, :, pl.ds(1, ROWS_Y - 1)], pick_recv.at[kv])

    alive = live[f, 1] > 0
    keys = levels * ROWS_Y * listed.shape[4]

    def bank_head(h, _):
        hs = pl.ds(pl.multiple_of(h * HEAD_DIM, HEAD_DIM), HEAD_DIM)
        for block in range(2):
            rows = spatial // 2
            q = qv[pl.ds(block * rows, rows), :, hs].reshape(rows * here, HEAD_DIM)
            s0 = dot_t(q, listed[0, 0, :, :, :, hs].reshape(keys, HEAD_DIM))
            s1 = dot_t(q, listed[0, 1, :, :, :, hs].reshape(keys, HEAD_DIM))
            peak1 = jnp.max(s1, axis=1, keepdims=True)
            peak = jnp.max(s0, axis=1, keepdims=True)
            peak = jnp.where(alive, jnp.maximum(peak, peak1), peak)
            p0 = jnp.exp2((s0 - peak) * EXP2_SCALE)
            p1 = jnp.exp2((s1 - jnp.where(alive, peak, FAR)) * EXP2_SCALE)
            total = jnp.sum(p0, axis=1, keepdims=True) + jnp.sum(p1, axis=1, keepdims=True)
            got = dot(p0.astype(jnp.bfloat16), listed[1, 0, :, :, :, hs].reshape(keys, HEAD_DIM))
            got += dot(p1.astype(jnp.bfloat16), listed[1, 1, :, :, :, hs].reshape(keys, HEAD_DIM))
            ref_out[pl.ds(block * rows * here, rows * here), hs] = got / total
        return 0

    lax.fori_loop(0, heads, bank_head, 0)

    keep.wait()
    await_bytes(qkv.at[:, :, pl.ds(1, shards - 1)], token_recv)

    def frame_head(h, _):
        hs = pl.ds(pl.multiple_of(h * HEAD_DIM, HEAD_DIM), HEAD_DIM)
        for s in range(mine):
            q, k, v = (qkv[i, s, :, :, hs].reshape(shards * here, HEAD_DIM) for i in range(3))
            scores = dot_t(q, k)
            peak = jnp.max(scores, axis=1, keepdims=True)
            p = jnp.exp2((scores - peak) * EXP2_SCALE)
            got = dot(p.astype(jnp.bfloat16), v) / jnp.sum(p, axis=1, keepdims=True)
            o_here[s, :, :, hs] = got.astype(jnp.bfloat16).reshape(shards, here, HEAD_DIM)
        return 0

    lax.fori_loop(0, heads, frame_head, 0)

    @pl.loop(1, shards)
    def _(i):
        p = peer(i)
        remote(o_here.at[:, p], o_back.at[pl.ds(mine * f, mine)], o_send, o_recv, frames=p)

    keep_o = pltpu.make_async_copy(o_here.at[:, f], o_back.at[pl.ds(mine * f, mine)], own_sem)
    keep_o.start()
    keep_o.wait()
    load_w.wait()
    await_bytes(o_back.at[pl.ds(0, mine * (shards - 1))], o_recv)

    group = spatial * here // chips
    rows = group // 2
    order = (lax.rem(x + 2, chips), lax.rem(x + 1, chips), lax.rem(x + chips - 1, chips), x)
    columns = weight.shape[1]
    tile = 640
    pairs = []
    for k, dest in enumerate(order):
        at = pl.multiple_of(dest * group, group)
        combined[...] = (
            ref_out[pl.ds(at, group), :]
            + o_back[pl.ds(pl.multiple_of(dest * (spatial // chips), spatial // chips), spatial // chips)]
            .reshape(group, width).astype(jnp.float32)
        ).astype(jnp.bfloat16)

        @pl.loop(0, columns // tile)
        def _(n):
            cs = pl.ds(pl.multiple_of(n * tile, tile), tile)
            part[k, :, :, cs] = dot(combined[...], wv[:, cs]).astype(jnp.bfloat16).reshape(2, rows, tile)

        pairs.append(remote(part.at[k, 1 - core], pair.at[k], pair_send.at[k], pair_recv.at[k], heads=twin))

    def total(k, n, *more):
        cs = pl.ds(pl.multiple_of(n * tile, tile), tile)
        value = part[k, core, :, cs].astype(jnp.float32) + pair[k, :, cs].astype(jnp.float32)
        return value, cs

    h2 = rows // 2
    pairs[0].wait_recv()

    @pl.loop(0, columns // tile)
    def _(n):
        value, cs = total(0, n)
        summed[0, :, cs] = value.astype(jnp.bfloat16)

    sums = [
        remote(summed.at[0, pl.ds(0, h2)], from_left_half, sum_send.at[0], sum_recv.at[0], heads=right),
        remote(summed.at[0, pl.ds(h2, h2)], from_right_half, sum_send.at[1], sum_recv.at[1], heads=left),
    ]
    for k in (1, 2):
        pairs[k].wait_recv()
        await_bytes((from_left_half, from_right_half)[k - 1], sum_recv.at[k - 1])

        @pl.loop(0, columns // tile)
        def _(n):
            value, cs = total(k, n)
            top, bottom = value[:h2], value[h2:]
            if k == 1:
                top += from_left_half[:, cs].astype(jnp.float32)
            else:
                bottom += from_right_half[:, cs].astype(jnp.float32)
            summed[k, pl.ds(0, h2), cs] = top.astype(jnp.bfloat16)
            summed[k, pl.ds(h2, h2), cs] = bottom.astype(jnp.bfloat16)

        sums.append(
            remote(summed.at[k], (from_left, from_right)[k - 1], sum_send.at[k + 1], sum_recv.at[k + 1],
                   heads=(right, left)[k - 1])
        )
    pairs[3].wait_recv()
    await_bytes(from_left, sum_recv.at[2])
    await_bytes(from_right, sum_recv.at[3])

    @pl.loop(0, columns // tile)
    def _(n):
        value, cs = total(3, n)
        value += from_left[:, cs].astype(jnp.float32)
        value += from_right[:, cs].astype(jnp.float32)
        out[:, cs] = value.astype(jnp.bfloat16)

    for copy in (*sends, *pairs, *sums):
        copy.wait_send()
    await_bytes(picked, pick_send)
    await_bytes(tokens.at[:, pl.ds(0, mine * (shards - 1))], token_send)
    await_bytes(o_back.at[pl.ds(0, mine * (shards - 1))], o_send)


def local(dims, bank_query, char_bank, char_slots, slot_live, frame_tokens, out_weight):
    shards, levels, chips = dims
    spatial, here, width = bank_query.shape
    _, characters, ref_here, _ = char_bank.shape
    mine = spatial // shards
    columns = out_weight.shape[1]
    group = spatial * here // chips
    rows = group // 2
    bf16, f32 = jnp.bfloat16, jnp.float32
    dma = pltpu.SemaphoreType.DMA
    scratch = [pltpu.VMEM((characters, ref_here, width), bf16) for _ in range(2 * levels)] + [
        pltpu.VMEM((2, levels, ROWS_Y - 1, 2, ref_here, width), bf16),
        pltpu.VMEM((2, 2, levels, ROWS_Y, ref_here, width), bf16),
        pltpu.VMEM((spatial, here, width), bf16),
        pltpu.VMEM((width, columns), bf16),
        pltpu.VMEM((3, mine, shards, here, width), bf16),
        pltpu.VMEM((mine, shards, here, width), bf16),
        pltpu.VMEM((spatial, here, width), bf16),
        pltpu.VMEM((spatial * here, width), f32),
        pltpu.VMEM((group, width), bf16),
        pltpu.VMEM((chips, 2, rows, columns), bf16),
        pltpu.VMEM((chips, rows, columns), bf16),
        pltpu.VMEM((3, rows, columns), bf16),
        pltpu.VMEM((rows // 2, columns), bf16),
        pltpu.VMEM((rows // 2, columns), bf16),
        pltpu.VMEM((rows, columns), bf16),
        pltpu.VMEM((rows, columns), bf16),
        dma((5,)), dma((2, levels)), dma((2, levels)), dma(()), dma((2,)), dma(()), dma(()), dma(()), dma(()),
        dma((chips,)), dma((chips,)), dma((4,)), dma((4,)), dma(()),
    ]
    smem = pl.BlockSpec(memory_space=pltpu.SMEM)
    anywhere = pl.BlockSpec(memory_space=pl.ANY)
    out = pl.pallas_call(
        functools.partial(kernel, dims),
        out_shape=jax.ShapeDtypeStruct((rows, columns), bf16),
        in_specs=[smem, smem, anywhere, anywhere, anywhere, anywhere],
        out_specs=pl.BlockSpec(memory_space=pltpu.VMEM),
        scratch_shapes=scratch,
        compiler_params=pltpu.CompilerParams(
            collective_id=0, has_side_effects=True, vmem_limit_bytes=60 * 1024 * 1024
        ),
        name="block",
    )(char_slots, slot_live, bank_query, char_bank, frame_tokens, out_weight)
    return out.reshape(rows // here, here, columns)


def solution(mesh):
    shards = mesh.shape["frames"]
    dims = (shards, shards // ROWS_Y, mesh.shape["heads"] // 2)
    in_specs = (
        P(None, "frames", "heads"),
        P(None, None, "frames", "heads"),
        P(),
        P(),
        P(None, None, "frames", "heads"),
        P("heads", None),
    )
    return jax.shard_map(
        functools.partial(local, dims), mesh=mesh, in_specs=in_specs, out_specs=P("heads", "frames", None), check_vma=False
    )
```

```python
import functools

import jax
import jax.numpy as jnp
from jax import lax
from jax.experimental import pallas as pl
from jax.experimental.pallas import tpu as pltpu
from jax.sharding import PartitionSpec as P

HEAD_DIM = 128
ROWS_Y = 4
CHUNKS = 4
EXP2_SCALE = HEAD_DIM ** -0.5 * 1.4426950408889634
FAR = 1e30
MESH = pl.DeviceIdType.MESH
scope = jax.named_scope


def dot_t(a, b):
    return lax.dot_general(a, b, (((1,), (1,)), ((), ())), preferred_element_type=jnp.float32)


def dot(a, b):
    return jnp.dot(a, b, preferred_element_type=jnp.float32)


def await_bytes(ref, sem):
    pltpu.make_async_copy(ref, ref, sem).wait()


def remote(src, dst, send, recv, **where):
    pltpu.make_async_remote_copy(
        src_ref=src, dst_ref=dst, send_sem=send, recv_sem=recv, device_id=where, device_id_type=MESH
    ).start()


def kernel(dims, slots, live, queries, bank, tokens, weight, out, *scratch):
    shards, levels, chips = dims
    held = (scratch[0:levels], scratch[levels:2 * levels])
    (picked, listed, qv, wv, qkv, o_here, o_back, ref_out, combined, part, pair, summed, half_l, half_r, full_l, full_r,
     local_sem, ring_send, ring_recv, pick_send, pick_recv, token_send, token_recv, o_send, o_recv, pair_send, pair_recv,
     half_send, half_recv, full_send, full_recv, own_sem) = scratch[2 * levels:]
    spatial, here, width = queries.shape
    heads = width // HEAD_DIM
    mine = spatial // shards
    half = levels // 2
    f = lax.axis_index("frames")
    r = lax.axis_index("heads")
    z, y = lax.div(f, ROWS_Y), lax.rem(f, ROWS_Y)
    x, core = lax.div(r, 2), lax.rem(r, 2)
    up = lax.rem(z + 1, levels) * ROWS_Y + y
    down = lax.rem(z + levels - 1, levels) * ROWS_Y + y
    twin = r + 1 - 2 * core
    right = lax.rem(x + 1, chips) * 2 + core
    left = lax.rem(x + chips - 1, chips) * 2 + core

    def peer(i):
        k, dy = lax.div(i, ROWS_Y), lax.rem(i, ROWS_Y)
        odd = lax.rem(k, 2)
        dz = odd * lax.div(k + 1, 2) + (1 - odd) * (levels - lax.div(k, 2))
        return lax.rem(z + dz, levels) * ROWS_Y + lax.rem(y + dy, ROWS_Y)

    own = [pltpu.make_async_copy(bank.at[kv], held[kv][0], local_sem.at[kv]) for kv in range(2)]
    load_q = pltpu.make_async_copy(queries, qv, local_sem.at[2])
    load_w = pltpu.make_async_copy(weight, wv, local_sem.at[3])
    keep = [pltpu.make_async_copy(tokens.at[:, mine * f + s], qkv.at[s, :, f], own_sem.at[0, s]) for s in range(mine)]
    for copy in (*own, load_q, *keep, load_w):
        copy.start()

    with scope("barrier"):
        barrier = pltpu.get_barrier_semaphore()

        @pl.loop(1, shards)
        def _(i):
            pl.semaphore_signal(barrier, inc=1, device_id={"frames": peer(i)}, device_id_type=MESH)

        for near in (twin, right, left):
            pl.semaphore_signal(barrier, inc=1, device_id={"heads": near}, device_id_type=MESH)
        pl.semaphore_wait(barrier, shards - 1 + 3)

    def pass_on(kv, src, rel, upward):
        ref = bank.at[kv] if src == 0 else held[kv][src]
        remote(ref, held[kv][rel], ring_send.at[kv, rel], ring_recv.at[kv, rel], frames=up if upward else down)

    def pick(kv, rel):
        for dy in range(ROWS_Y):
            shard = z * ROWS_Y + lax.rem(y + dy, ROWS_Y)
            for j in range(2):
                block = held[kv][rel][slots[j, shard]]
                if dy:
                    picked[kv, rel, dy - 1, j] = block
                else:
                    listed[kv, j, rel, 0] = block
        for dy in range(1, ROWS_Y):
            remote(
                picked.at[kv, rel, dy - 1], listed.at[kv, :, rel, dy], pick_send, pick_recv.at[kv],
                frames=z * ROWS_Y + lax.rem(y + dy, ROWS_Y),
            )

    def send_tokens(s, first, last):
        @pl.loop(first, last)
        def _(i):
            p = peer(i)
            remote(tokens.at[:, mine * p + s], qkv.at[s, :, f], token_send, token_recv.at[s], frames=p)

    def frame_attention(s):
        with scope(f"wait_tokens{s}"):
            keep[s].wait()
            await_bytes(qkv.at[s, :, pl.ds(1, shards - 1)], token_recv.at[s])

        def head(h, _):
            hs = pl.ds(pl.multiple_of(h * HEAD_DIM, HEAD_DIM), HEAD_DIM)
            q, k, v = (qkv[s, i, :, :, hs].reshape(shards * here, HEAD_DIM) for i in range(3))
            scores = dot_t(q, k)
            peak = jnp.max(scores, axis=1, keepdims=True)
            p = jnp.exp2((scores - peak) * EXP2_SCALE)
            got = dot(p.astype(jnp.bfloat16), v) / jnp.sum(p, axis=1, keepdims=True)
            o_here[s, :, :, hs] = got.astype(jnp.bfloat16).reshape(shards, here, HEAD_DIM)
            return 0

        with scope(f"frame_attention{s}"):
            lax.fori_loop(0, heads, head, 0)

        @pl.loop(1, shards)
        def _(i):
            p = peer(i)
            remote(o_here.at[s, p], o_back.at[s, f], o_send, o_recv.at[s], frames=p)

        pltpu.make_async_copy(o_here.at[s, f], o_back.at[s, f], own_sem.at[1, s]).start()

    alive = live[1, f] > 0
    keys = levels * ROWS_Y * listed.shape[4]

    def bank_head(h, _):
        hs = pl.ds(pl.multiple_of(h * HEAD_DIM, HEAD_DIM), HEAD_DIM)
        for block in range(2):
            rows = spatial // 2
            q = qv[pl.ds(block * rows, rows), :, hs].reshape(rows * here, HEAD_DIM)
            s0 = dot_t(q, listed[0, 0, :, :, :, hs].reshape(keys, HEAD_DIM))
            s1 = dot_t(q, listed[0, 1, :, :, :, hs].reshape(keys, HEAD_DIM))
            peak1 = jnp.max(s1, axis=1, keepdims=True)
            peak = jnp.max(s0, axis=1, keepdims=True)
            peak = jnp.where(alive, jnp.maximum(peak, peak1), peak)
            p0 = jnp.exp2((s0 - peak) * EXP2_SCALE)
            p1 = jnp.exp2((s1 - jnp.where(alive, peak, FAR)) * EXP2_SCALE)
            total = jnp.sum(p0, axis=1, keepdims=True) + jnp.sum(p1, axis=1, keepdims=True)
            got = dot(p0.astype(jnp.bfloat16), listed[1, 0, :, :, :, hs].reshape(keys, HEAD_DIM))
            got += dot(p1.astype(jnp.bfloat16), listed[1, 1, :, :, :, hs].reshape(keys, HEAD_DIM))
            ref_out[pl.ds(block * rows // mine, rows // mine), :, :, hs] = (got / total).reshape(
                rows // mine, mine, here, HEAD_DIM
            )
        return 0

    order = (lax.rem(x + 2, chips), lax.rem(x + 1, chips), lax.rem(x + chips - 1, chips), x)
    homes = shards // chips
    rows = homes * here // 2
    h2 = rows // 2
    chunk = weight.shape[1] // CHUNKS
    tile = chunk // 2

    def project(s):
        with scope(f"wait_o{s}"):
            pltpu.make_async_copy(o_here.at[s, f], o_back.at[s, f], own_sem.at[1, s]).wait()
            await_bytes(o_back.at[s, pl.ds(1, shards - 1)], o_recv.at[s])
        with scope(f"project{s}"):
            for k, dest in enumerate(order):
                at = pl.ds(pl.multiple_of(dest * homes, homes), homes)
                combined[pl.ds(k * 2 * rows, 2 * rows), :] = (
                    (ref_out[at, s] + o_back[s, at].astype(jnp.float32)).astype(jnp.bfloat16).reshape(2 * rows, width)
                )

            @pl.loop(0, CHUNKS)
            def _(n):
                for t in range(2):
                    cs = pl.ds(pl.multiple_of(n * chunk + t * tile, tile), tile)
                    part[s, n, :, :, :, pl.ds(t * tile, tile)] = (
                        dot(combined[...], wv[:, cs]).astype(jnp.bfloat16).reshape(chips, 2, rows, tile)
                    )
                remote(part.at[s, n, :, 1 - core], pair.at[s, n], pair_send, pair_recv.at[s, n], heads=twin)

    def both(s, n, k):
        return part[s, n, k, core].astype(jnp.float32) + pair[s, n, k].astype(jnp.float32)

    def first_hop(s):
        with scope(f"first_hop{s}"):
            @pl.loop(0, CHUNKS)
            def _(n):
                await_bytes(pair.at[s, n], pair_recv.at[s, n])
                summed[s, n, 0] = both(s, n, 0).astype(jnp.bfloat16)
                remote(summed.at[s, n, 0, pl.ds(0, h2)], half_l.at[s, n], half_send, half_recv.at[0, s, n], heads=right)
                remote(summed.at[s, n, 0, pl.ds(h2, h2)], half_r.at[s, n], half_send, half_recv.at[1, s, n], heads=left)

    def second_hop(s):
        with scope(f"second_hop{s}"):
            @pl.loop(0, CHUNKS)
            def _(n):
                await_bytes(half_l.at[s, n], half_recv.at[0, s, n])
                value = both(s, n, 1)
                top = value[:h2] + half_l[s, n].astype(jnp.float32)
                summed[s, n, 1, pl.ds(0, h2)] = top.astype(jnp.bfloat16)
                summed[s, n, 1, pl.ds(h2, h2)] = value[h2:].astype(jnp.bfloat16)
                remote(summed.at[s, n, 1], full_l.at[s, n], full_send, full_recv.at[0, s, n], heads=right)
                await_bytes(half_r.at[s, n], half_recv.at[1, s, n])
                value = both(s, n, 2)
                low = value[h2:] + half_r[s, n].astype(jnp.float32)
                summed[s, n, 2, pl.ds(0, h2)] = value[:h2].astype(jnp.bfloat16)
                summed[s, n, 2, pl.ds(h2, h2)] = low.astype(jnp.bfloat16)
                remote(summed.at[s, n, 2], full_r.at[s, n], full_send, full_recv.at[1, s, n], heads=left)

    def finish(s):
        with scope(f"finish{s}"):
            @pl.loop(0, CHUNKS)
            def _(n):
                await_bytes(full_l.at[s, n], full_recv.at[0, s, n])
                await_bytes(full_r.at[s, n], full_recv.at[1, s, n])
                value = both(s, n, 3) + full_l[s, n].astype(jnp.float32) + full_r[s, n].astype(jnp.float32)
                cs = pl.ds(pl.multiple_of(n * chunk, chunk), chunk)
                out[:, s, :, cs] = value.astype(jnp.bfloat16).reshape(homes // 2, here, chunk)

    with scope("own"):
        for kv in range(2):
            pass_on(kv, 0, 1, True)
            pass_on(kv, 0, levels - 1, False)
        for kv in range(2):
            own[kv].wait()
            pick(kv, 0)
    middle = shards // 2
    for step in range(1, half + 1):
        if step == half:
            send_tokens(0, 1, shards)
            send_tokens(1, 1, middle)
        with scope(f"ring{step}"):
            for kv in range(2):
                for rel, upward in ((step, True), (levels - step, False)):
                    if step == half and upward != (kv == 0):
                        continue
                    await_bytes(held[kv][rel], ring_recv.at[kv, rel])
                    last = half if upward == (kv == 0) else half - 1
                    if step < last:
                        pass_on(kv, rel, rel + 1 if upward else rel - 1, upward)
                    pick(kv, rel)

    frame_attention(0)
    send_tokens(1, middle, shards)
    with scope("wait_picks"):
        load_q.wait()
        for kv in range(2):
            await_bytes(listed.at[kv, :, :, pl.ds(1, ROWS_Y - 1)], pick_recv.at[kv])
    with scope("bank_attention"):
        lax.fori_loop(0, heads, bank_head, 0)
    load_w.wait()
    project(0)
    first_hop(0)
    frame_attention(1)
    second_hop(0)
    project(1)
    first_hop(1)
    finish(0)
    second_hop(1)
    finish(1)

    with scope("drain"):
        for kv in range(2):
            for rel in range(1, levels):
                await_bytes(held[kv][rel], ring_send.at[kv, rel])
        await_bytes(picked, pick_send)
        for s in range(mine):
            await_bytes(qkv.at[s, :, pl.ds(1, shards - 1)], token_send)
            await_bytes(o_back.at[s, pl.ds(1, shards - 1)], o_send)
        await_bytes(pair, pair_send)
        await_bytes(half_l, half_send)
        await_bytes(half_r, half_send)
        await_bytes(full_l, full_send)
        await_bytes(full_r, full_send)


def local(dims, bank_query, char_bank, char_slots, slot_live, frame_tokens, out_weight):
    shards, levels, chips = dims
    spatial, here, width = bank_query.shape
    _, characters, ref_here, _ = char_bank.shape
    mine = spatial // shards
    columns = out_weight.shape[1]
    homes = shards // chips
    rows = homes * here // 2
    chunk = columns // CHUNKS
    bf16, f32 = jnp.bfloat16, jnp.float32
    dma = pltpu.SemaphoreType.DMA
    vmem = pltpu.VMEM
    scratch = [vmem((characters, ref_here, width), bf16) for _ in range(2 * levels)] + [
        vmem((2, levels, ROWS_Y - 1, 2, ref_here, width), bf16),
        vmem((2, 2, levels, ROWS_Y, ref_here, width), bf16),
        vmem((spatial, here, width), bf16),
        vmem((width, columns), bf16),
        vmem((mine, 3, shards, here, width), bf16),
        vmem((mine, shards, here, width), bf16),
        vmem((mine, shards, here, width), bf16),
        vmem((shards, mine, here, width), f32),
        vmem((shards * here, width), bf16),
        vmem((mine, CHUNKS, chips, 2, rows, chunk), bf16),
        vmem((mine, CHUNKS, chips, rows, chunk), bf16),
        vmem((mine, CHUNKS, 3, rows, chunk), bf16),
        vmem((mine, CHUNKS, rows // 2, chunk), bf16),
        vmem((mine, CHUNKS, rows // 2, chunk), bf16),
        vmem((mine, CHUNKS, rows, chunk), bf16),
        vmem((mine, CHUNKS, rows, chunk), bf16),
        dma((4,)), dma((2, levels)), dma((2, levels)), dma(()), dma((2,)), dma(()), dma((mine,)), dma(()), dma((mine,)),
        dma(()), dma((mine, CHUNKS)), dma(()), dma((2, mine, CHUNKS)), dma(()), dma((2, mine, CHUNKS)), dma((2, mine)),
    ]
    smem = pl.BlockSpec(memory_space=pltpu.SMEM)
    anywhere = pl.BlockSpec(memory_space=pl.ANY)
    out = pl.pallas_call(
        functools.partial(kernel, dims),
        out_shape=jax.ShapeDtypeStruct((homes // 2, mine, here, columns), bf16),
        in_specs=[smem, smem, anywhere, anywhere, anywhere, anywhere],
        out_specs=pl.BlockSpec(memory_space=pltpu.VMEM),
        scratch_shapes=scratch,
        compiler_params=pltpu.CompilerParams(
            collective_id=0, has_side_effects=True, vmem_limit_bytes=60 * 1024 * 1024
        ),
        name="block",
    )(char_slots.T, slot_live.T, bank_query, char_bank, frame_tokens, out_weight)
    return out.reshape(homes // 2 * mine, here, columns)


def solution(mesh):
    shards = mesh.shape["frames"]
    dims = (shards, shards // ROWS_Y, mesh.shape["heads"] // 2)
    in_specs = (
        P(None, "frames", "heads"),
        P(None, None, "frames", "heads"),
        P(),
        P(),
        P(None, None, "frames", "heads"),
        P("heads", None),
    )
    return jax.shard_map(
        functools.partial(local, dims), mesh=mesh, in_specs=in_specs, out_specs=P("heads", "frames", None), check_vma=False
    )
```

```python
import functools

import jax
import jax.numpy as jnp
from jax import lax
from jax.experimental import pallas as pl
from jax.experimental.pallas import tpu as pltpu
from jax.sharding import PartitionSpec as P

HEAD_DIM = 128
ROWS_Y = 4
CHUNKS = 4
UNITS = 3
EARLY = 4
AHEAD = 6
LAG = 2
EXP2_SCALE = HEAD_DIM ** -0.5 * 1.4426950408889634
FAR = 1e30
MESH = pl.DeviceIdType.MESH
scope = jax.named_scope


def dot_t(a, b):
    return lax.dot_general(a, b, (((1,), (1,)), ((), ())), preferred_element_type=jnp.float32)


def dot(a, b):
    return jnp.dot(a, b, preferred_element_type=jnp.float32)


def await_bytes(ref, sem):
    pltpu.make_async_copy(ref, ref, sem).wait()


def remote(src, dst, send, recv, **where):
    pltpu.make_async_remote_copy(
        src_ref=src, dst_ref=dst, send_sem=send, recv_sem=recv, device_id=where, device_id_type=MESH
    ).start()


def unit_rows(u, here):
    return here * (ROWS_Y if u == 0 else ROWS_Y // 2)


def kernel(dims, slots, live, queries, bank, tokens, weight, out, *scratch):
    shards, levels, chips = dims
    held = (scratch[0:levels], scratch[levels:2 * levels])
    (picked, listed, qv, wv, qkv, o_here, o_back, ref_out, combined) = scratch[2 * levels:2 * levels + 9]
    buffers = scratch[2 * levels + 9:-16]
    part, pair, summed, half_l, half_r, full_l, full_r = (buffers[i * UNITS:(i + 1) * UNITS] for i in range(7))
    (local_sem, ring_send, ring_recv, pick_send, pick_recv, token_send, token_recv, o_send, o_recv, pair_send, pair_recv,
     half_send, half_recv, full_send, full_recv, own_sem) = scratch[-16:]
    spatial, here, width = queries.shape
    heads = width // HEAD_DIM
    mine = spatial // shards
    half = levels // 2
    f = lax.axis_index("frames")
    r = lax.axis_index("heads")
    z, y = lax.div(f, ROWS_Y), lax.rem(f, ROWS_Y)
    x, core = lax.div(r, 2), lax.rem(r, 2)
    up = lax.rem(z + 1, levels) * ROWS_Y + y
    down = lax.rem(z + levels - 1, levels) * ROWS_Y + y
    twin = r + 1 - 2 * core
    right = lax.rem(x + 1, chips) * 2 + core
    left = lax.rem(x + chips - 1, chips) * 2 + core

    colour = lax.rem(z + y, 2)

    def place(k, dy):
        odd = lax.rem(k, 2)
        dz = odd * lax.div(k + 1, 2) + (1 - odd) * (levels - lax.div(k, 2))
        return lax.rem(z + dz, levels), lax.rem(y + dy, ROWS_Y)

    def peer(i):
        there_z, there_y = place(lax.div(i, ROWS_Y), lax.rem(i, ROWS_Y))
        return there_z * ROWS_Y + there_y

    def peer_of(i, wanted):
        there_z, _ = place(lax.div(i, 2), 0)
        dy = lax.rem(there_z + y + wanted, 2) + 2 * lax.rem(i, 2)
        return there_z * ROWS_Y + lax.rem(y + dy, ROWS_Y)

    own = [pltpu.make_async_copy(bank.at[kv], held[kv][0], local_sem.at[kv]) for kv in range(2)]
    load_q = pltpu.make_async_copy(queries, qv, local_sem.at[2])
    load_w = pltpu.make_async_copy(weight, wv, local_sem.at[3])
    keep = [pltpu.make_async_copy(tokens.at[:, mine * f + s], qkv.at[s, :, f], own_sem.at[0, s]) for s in range(mine)]
    for copy in (*own, load_q, *keep, load_w):
        copy.start()

    with scope("barrier"):
        barrier = pltpu.get_barrier_semaphore()

        @pl.loop(1, shards)
        def _(i):
            pl.semaphore_signal(barrier, inc=1, device_id={"frames": peer(i)}, device_id_type=MESH)

        for near in (twin, right, left):
            pl.semaphore_signal(barrier, inc=1, device_id={"heads": near}, device_id_type=MESH)
        pl.semaphore_wait(barrier, shards - 1 + 3)

    def pass_on(kv, src, rel, upward):
        ref = bank.at[kv] if src == 0 else held[kv][src]
        remote(ref, held[kv][rel], ring_send.at[kv, rel], ring_recv.at[kv, rel], frames=up if upward else down)

    def pick(kv, rel):
        for dy in range(ROWS_Y):
            shard = z * ROWS_Y + lax.rem(y + dy, ROWS_Y)
            for j in range(2):
                block = held[kv][rel][slots[j, shard]]
                if dy:
                    picked[kv, rel, dy - 1, j] = block
                else:
                    listed[kv, j, rel, 0] = block
        for dy in range(1, ROWS_Y):
            remote(
                picked.at[kv, rel, dy - 1], listed.at[kv, :, rel, dy], pick_send, pick_recv.at[kv],
                frames=z * ROWS_Y + lax.rem(y + dy, ROWS_Y),
            )

    def send_tokens(s, first, last):
        @pl.loop(first, last)
        def _(i):
            p = peer(i)
            remote(tokens.at[:, mine * p + s], qkv.at[s, :, f], token_send, token_recv.at[s], frames=p)

    def send_coloured(s, wanted, first, last):
        @pl.loop(first if first else lax.rem(colour + wanted + 1, 2), last)
        def _(i):
            p = peer_of(i, wanted)
            remote(tokens.at[:, mine * p + s], qkv.at[s, :, f], token_send, token_recv.at[s], frames=p)

    def frame_attention(s):
        unit = s * (1 + colour)

        with scope(f"wait_tokens{s}"):
            keep[s].wait()
            await_bytes(qkv.at[s, :, pl.ds(1, shards - 1)], token_recv.at[s])

        def head(h, _):
            hs = pl.ds(pl.multiple_of(h * HEAD_DIM, HEAD_DIM), HEAD_DIM)
            q, k, v = (qkv[s, i, :, :, hs].reshape(shards * here, HEAD_DIM) for i in range(3))
            scores = dot_t(q, k)
            peak = jnp.max(scores, axis=1, keepdims=True)
            p = jnp.exp2((scores - peak) * EXP2_SCALE)
            got = dot(p.astype(jnp.bfloat16), v) / jnp.sum(p, axis=1, keepdims=True)
            o_here[s, :, :, hs] = got.astype(jnp.bfloat16).reshape(shards, here, HEAD_DIM)
            return 0

        with scope(f"frame_attention{s}"):
            lax.fori_loop(0, heads, head, 0)

        @pl.loop(1, shards)
        def _(i):
            p = peer(i)
            remote(o_here.at[s, p], o_back.at[s, f], o_send, o_recv.at[unit], frames=p)

        pltpu.make_async_copy(o_here.at[s, f], o_back.at[s, f], o_recv.at[unit]).start()

    alive = live[1, f] > 0
    keys = levels * ROWS_Y * listed.shape[4]

    def bank_head(h, _):
        hs = pl.ds(pl.multiple_of(h * HEAD_DIM, HEAD_DIM), HEAD_DIM)
        for block in range(2):
            rows = spatial // 2
            q = qv[pl.ds(block * rows, rows), :, hs].reshape(rows * here, HEAD_DIM)
            s0 = dot_t(q, listed[0, 0, :, :, :, hs].reshape(keys, HEAD_DIM))
            s1 = dot_t(q, listed[0, 1, :, :, :, hs].reshape(keys, HEAD_DIM))
            peak1 = jnp.max(s1, axis=1, keepdims=True)
            peak = jnp.max(s0, axis=1, keepdims=True)
            peak = jnp.where(alive, jnp.maximum(peak, peak1), peak)
            p0 = jnp.exp2((s0 - peak) * EXP2_SCALE)
            p1 = jnp.exp2((s1 - jnp.where(alive, peak, FAR)) * EXP2_SCALE)
            total = jnp.sum(p0, axis=1, keepdims=True) + jnp.sum(p1, axis=1, keepdims=True)
            got = dot(p0.astype(jnp.bfloat16), listed[1, 0, :, :, :, hs].reshape(keys, HEAD_DIM))
            got += dot(p1.astype(jnp.bfloat16), listed[1, 1, :, :, :, hs].reshape(keys, HEAD_DIM))
            ref_out[pl.ds(block * rows // mine, rows // mine), :, :, hs] = (got / total).reshape(
                rows // mine, mine, here, HEAD_DIM
            )
        return 0

    order = (lax.rem(x + 2, chips), lax.rem(x + 1, chips), lax.rem(x + chips - 1, chips), x)
    homes = shards // chips
    chunk = weight.shape[1] // CHUNKS
    tile = chunk // 2

    def project(u):
        s = min(u, 1)
        rows = unit_rows(u, here)
        with scope(f"wait_o{u}"):
            await_bytes(o_back.at[s, pl.ds(0, shards if u == 0 else shards // 2)], o_recv.at[u])
        with scope(f"project{u}"):
            for k, dest in enumerate(order):
                for c in range(2):
                    base = pl.multiple_of(dest * homes, homes) + c * ROWS_Y
                    at = (k * 2 + c) * rows
                    if u == 0:
                        span = pl.ds(base, ROWS_Y)
                        value = ref_out[span, s] + o_back[s, span].astype(jnp.float32)
                        combined[pl.ds(at, rows), :] = value.astype(jnp.bfloat16).reshape(rows, width)
                        continue
                    for j in range(2):
                        p = base + (u - 1 + c) % 2 + 2 * j
                        value = ref_out[p, s] + o_back[s, p].astype(jnp.float32)
                        combined[pl.ds(at + j * here, here), :] = value.astype(jnp.bfloat16)
            for n in range(CHUNKS + LAG):
                if n < CHUNKS:
                    for t in range(2):
                        cs = pl.ds(n * chunk + t * tile, tile)
                        part[u][n, :, :, :, pl.ds(t * tile, tile)] = (
                            dot(combined[pl.ds(0, chips * 2 * rows), :], wv[:, cs])
                            .astype(jnp.bfloat16).reshape(chips, 2, rows, tile)
                        )
                    remote(part[u].at[n, :, 1 - core], pair[u].at[n], pair_send, pair_recv.at[u, n], heads=twin)
                if n >= LAG and u:
                    first_hop(u, n - LAG)

    def both(u, n, k):
        return part[u][n, k, core].astype(jnp.float32) + pair[u][n, k].astype(jnp.float32)

    def first_hop(u, n):
        h2 = unit_rows(u, here) // 2
        await_bytes(pair[u].at[n], pair_recv.at[u, n])
        summed[u][n, 0] = both(u, n, 0).astype(jnp.bfloat16)
        remote(summed[u].at[n, 0, pl.ds(0, h2)], half_l[u].at[n], half_send, half_recv.at[0, u, n], heads=right)
        remote(summed[u].at[n, 0, pl.ds(h2, h2)], half_r[u].at[n], half_send, half_recv.at[1, u, n], heads=left)

    def second_hop(u):
        h2 = unit_rows(u, here) // 2
        with scope(f"second_hop{u}"):
            @pl.loop(0, CHUNKS)
            def _(n):
                await_bytes(half_l[u].at[n], half_recv.at[0, u, n])
                value = both(u, n, 1)
                top = value[:h2] + half_l[u][n].astype(jnp.float32)
                summed[u][n, 1, pl.ds(0, h2)] = top.astype(jnp.bfloat16)
                summed[u][n, 1, pl.ds(h2, h2)] = value[h2:].astype(jnp.bfloat16)
                remote(summed[u].at[n, 1], full_l[u].at[n], full_send, full_recv.at[0, u, n], heads=right)
                await_bytes(half_r[u].at[n], half_recv.at[1, u, n])
                value = both(u, n, 2)
                low = value[h2:] + half_r[u][n].astype(jnp.float32)
                summed[u][n, 2, pl.ds(0, h2)] = value[:h2].astype(jnp.bfloat16)
                summed[u][n, 2, pl.ds(h2, h2)] = low.astype(jnp.bfloat16)
                remote(summed[u].at[n, 2], full_r[u].at[n], full_send, full_recv.at[1, u, n], heads=left)

    def finish(u):
        with scope(f"finish{u}"):
            @pl.loop(0, CHUNKS)
            def _(n):
                await_bytes(full_l[u].at[n], full_recv.at[0, u, n])
                await_bytes(full_r[u].at[n], full_recv.at[1, u, n])
                value = both(u, n, 3) + full_l[u][n].astype(jnp.float32) + full_r[u][n].astype(jnp.float32)
                value = value.astype(jnp.bfloat16)
                cs = pl.ds(pl.multiple_of(n * chunk, chunk), chunk)
                if u == 0:
                    out[:, 0, :, cs] = value.reshape(ROWS_Y, here, chunk)
                else:
                    for j in range(2):
                        out[lax.rem(u - 1 + core, 2) + 2 * j, 1, :, cs] = value[j * here:(j + 1) * here]

    with scope("own"):
        for kv in range(2):
            pass_on(kv, 0, 1, True)
            pass_on(kv, 0, levels - 1, False)
        send_tokens(0, 1, EARLY)
        for kv in range(2):
            own[kv].wait()
            pick(kv, 0)
    for step in range(1, half + 1):
        if step == half:
            send_tokens(0, EARLY, shards)
            send_coloured(1, 0, 0, AHEAD)
        with scope(f"ring{step}"):
            for kv in range(2):
                for rel, upward in ((step, True), (levels - step, False)):
                    if step == half and upward != (kv == 0):
                        continue
                    await_bytes(held[kv][rel], ring_recv.at[kv, rel])
                    last = half if upward == (kv == 0) else half - 1
                    if step < last:
                        pass_on(kv, rel, rel + 1 if upward else rel - 1, upward)
                    pick(kv, rel)

    frame_attention(0)
    send_coloured(1, 0, AHEAD, shards // 2)
    send_coloured(1, 1, 0, shards // 2)
    with scope("wait_picks"):
        load_q.wait()
        for kv in range(2):
            await_bytes(listed.at[kv, :, :, pl.ds(1, ROWS_Y - 1)], pick_recv.at[kv])
    with scope("bank_attention"):
        lax.fori_loop(0, heads, bank_head, 0)
    load_w.wait()
    project(0)

    with scope("first_hop0"):
        for n in range(CHUNKS):
            first_hop(0, n)

    @pl.when(colour == 0)
    def _():
        frame_attention(1)

    second_hop(0)

    @pl.when(colour == 1)
    def _():
        frame_attention(1)

    project(1)
    finish(0)
    second_hop(1)
    project(2)
    finish(1)
    second_hop(2)
    finish(2)

    with scope("drain"):
        for kv in range(2):
            for rel in range(1, levels):
                await_bytes(held[kv][rel], ring_send.at[kv, rel])
        await_bytes(picked, pick_send)
        for s in range(mine):
            await_bytes(qkv.at[s, :, pl.ds(1, shards - 1)], token_send)
            await_bytes(o_back.at[s, pl.ds(1, shards - 1)], o_send)
        for u in range(UNITS):
            await_bytes(pair[u], pair_send)
            await_bytes(half_l[u], half_send)
            await_bytes(half_r[u], half_send)
            await_bytes(full_l[u], full_send)
            await_bytes(full_r[u], full_send)


def local(dims, bank_query, char_bank, char_slots, slot_live, frame_tokens, out_weight):
    shards, levels, chips = dims
    spatial, here, width = bank_query.shape
    _, characters, ref_here, _ = char_bank.shape
    mine = spatial // shards
    columns = out_weight.shape[1]
    homes = shards // chips
    chunk = columns // CHUNKS
    rows = [unit_rows(u, here) for u in range(UNITS)]
    bf16, f32 = jnp.bfloat16, jnp.float32
    dma = pltpu.SemaphoreType.DMA
    vmem = pltpu.VMEM
    scratch = [vmem((characters, ref_here, width), bf16) for _ in range(2 * levels)] + [
        vmem((2, levels, ROWS_Y - 1, 2, ref_here, width), bf16),
        vmem((2, 2, levels, ROWS_Y, ref_here, width), bf16),
        vmem((spatial, here, width), bf16),
        vmem((width, columns), bf16),
        vmem((mine, 3, shards, here, width), bf16),
        vmem((mine, shards, here, width), bf16),
        vmem((mine, shards, here, width), bf16),
        vmem((shards, mine, here, width), f32),
        vmem((shards * here, width), bf16),
        *[vmem((CHUNKS, chips, 2, n, chunk), bf16) for n in rows],
        *[vmem((CHUNKS, chips, n, chunk), bf16) for n in rows],
        *[vmem((CHUNKS, 3, n, chunk), bf16) for n in rows],
        *[vmem((CHUNKS, n // 2, chunk), bf16) for n in rows * 2],
        *[vmem((CHUNKS, n, chunk), bf16) for n in rows * 2],
        dma((4,)), dma((2, levels)), dma((2, levels)), dma(()), dma((2,)), dma(()), dma((mine,)), dma(()), dma((UNITS,)),
        dma(()), dma((UNITS, CHUNKS)), dma(()), dma((2, UNITS, CHUNKS)), dma(()), dma((2, UNITS, CHUNKS)), dma((1, mine)),
    ]
    smem = pl.BlockSpec(memory_space=pltpu.SMEM)
    anywhere = pl.BlockSpec(memory_space=pl.ANY)
    out = pl.pallas_call(
        functools.partial(kernel, dims),
        out_shape=jax.ShapeDtypeStruct((homes // 2, mine, here, columns), bf16),
        in_specs=[smem, smem, anywhere, anywhere, anywhere, anywhere],
        out_specs=pl.BlockSpec(memory_space=pltpu.VMEM),
        scratch_shapes=scratch,
        compiler_params=pltpu.CompilerParams(
            collective_id=0, has_side_effects=True, vmem_limit_bytes=60 * 1024 * 1024
        ),
        name="block",
    )(char_slots.T, slot_live.T, bank_query, char_bank, frame_tokens, out_weight)
    return out.reshape(homes // 2 * mine, here, columns)


def solution(mesh):
    shards = mesh.shape["frames"]
    dims = (shards, shards // ROWS_Y, mesh.shape["heads"] // 2)
    in_specs = (
        P(None, "frames", "heads"),
        P(None, None, "frames", "heads"),
        P(),
        P(),
        P(None, None, "frames", "heads"),
        P("heads", None),
    )
    return jax.shard_map(
        functools.partial(local, dims), mesh=mesh, in_specs=in_specs, out_specs=P("heads", "frames", None), check_vma=False
    )
```

```python
import functools

import jax
import jax.numpy as jnp
from jax import lax
from jax.experimental import pallas as pl
from jax.experimental.pallas import tpu as pltpu
from jax.sharding import PartitionSpec as P

HEAD_DIM = 128
ROWS_Y = 4
CHUNKS = 4
UNITS = 3
EARLY = 4
AHEAD = 6
LAG = 2
START = 2
EXP2_SCALE = HEAD_DIM ** -0.5 * 1.4426950408889634
FAR = 1e30
MESH = pl.DeviceIdType.MESH
scope = jax.named_scope


def dot_t(a, b):
    return lax.dot_general(a, b, (((1,), (1,)), ((), ())), preferred_element_type=jnp.float32)


def dot(a, b):
    return jnp.dot(a, b, preferred_element_type=jnp.float32)


def await_bytes(ref, sem):
    pltpu.make_async_copy(ref, ref, sem).wait()


def remote(src, dst, send, recv, **where):
    pltpu.make_async_remote_copy(
        src_ref=src, dst_ref=dst, send_sem=send, recv_sem=recv, device_id=where, device_id_type=MESH
    ).start()


def unit_rows(u, here):
    return here * (ROWS_Y if u == 0 else ROWS_Y // 2)


def kernel(dims, slots, live, queries, bank, tokens, weight, out_hbm, *scratch):
    shards, levels, chips = dims
    held = (scratch[0:levels], scratch[levels:2 * levels])
    (picked, listed, qv, wv, qkv, o_here, o_back, ref_out, combined, out) = scratch[2 * levels:2 * levels + 10]
    buffers = scratch[2 * levels + 10:-17]
    part, pair, summed, half_l, half_r, full_l, full_r = (buffers[i * UNITS:(i + 1) * UNITS] for i in range(7))
    (local_sem, ring_send, ring_recv, pick_send, pick_recv, token_send, token_recv, o_send, o_recv, pair_send, pair_recv,
     half_send, half_recv, full_send, full_recv, own_sem, out_sem) = scratch[-17:]
    spatial, here, width = queries.shape
    heads = width // HEAD_DIM
    mine = spatial // shards
    half = levels // 2
    f = lax.axis_index("frames")
    r = lax.axis_index("heads")
    z, y = lax.div(f, ROWS_Y), lax.rem(f, ROWS_Y)
    x, core = lax.div(r, 2), lax.rem(r, 2)
    up = lax.rem(z + 1, levels) * ROWS_Y + y
    down = lax.rem(z + levels - 1, levels) * ROWS_Y + y
    twin = r + 1 - 2 * core
    right = lax.rem(x + 1, chips) * 2 + core
    left = lax.rem(x + chips - 1, chips) * 2 + core

    colour = lax.rem(z + y, 2)

    def place(k, dy):
        odd = lax.rem(k, 2)
        dz = odd * lax.div(k + 1, 2) + (1 - odd) * (levels - lax.div(k, 2))
        return lax.rem(z + dz, levels), lax.rem(y + dy, ROWS_Y)

    def peer(i):
        i = shards - i
        there_z, there_y = place(lax.div(i, ROWS_Y), lax.rem(i, ROWS_Y))
        return there_z * ROWS_Y + there_y

    def peer_of(i, wanted):
        there_z, _ = place(lax.div(i, 2), 0)
        dy = lax.rem(there_z + y + wanted, 2) + 2 * lax.rem(i, 2)
        return there_z * ROWS_Y + lax.rem(y + dy, ROWS_Y)

    own = [pltpu.make_async_copy(bank.at[kv], held[kv][0], local_sem.at[kv]) for kv in range(2)]
    load_q = pltpu.make_async_copy(queries, qv, local_sem.at[2])
    load_w = pltpu.make_async_copy(weight, wv, local_sem.at[3])
    keep = [pltpu.make_async_copy(tokens.at[:, mine * f + s], qkv.at[s, :, f], own_sem.at[0, s]) for s in range(mine)]
    for copy in (*own, load_q, *keep, load_w):
        copy.start()

    with scope("barrier"):
        barrier = pltpu.get_barrier_semaphore()

        @pl.loop(1, shards)
        def _(i):
            pl.semaphore_signal(barrier, inc=1, device_id={"frames": peer(i)}, device_id_type=MESH)

        for near in (twin, right, left):
            pl.semaphore_signal(barrier, inc=1, device_id={"heads": near}, device_id_type=MESH)
        pl.semaphore_wait(barrier, shards - 1 + 3)

    def pass_on(kv, src, rel, upward):
        ref = bank.at[kv] if src == 0 else held[kv][src]
        remote(ref, held[kv][rel], ring_send.at[kv, rel], ring_recv.at[kv, rel], frames=up if upward else down)

    def pick(kv, rel):
        for dy in range(ROWS_Y):
            shard = z * ROWS_Y + lax.rem(y + dy, ROWS_Y)
            for j in range(2):
                block = held[kv][rel][slots[j, shard]]
                if dy:
                    picked[kv, rel, dy - 1, j] = block
                else:
                    listed[kv, j, rel, 0] = block
        for dy in range(1, ROWS_Y):
            remote(
                picked.at[kv, rel, dy - 1], listed.at[kv, :, rel, dy], pick_send, pick_recv.at[kv],
                frames=z * ROWS_Y + lax.rem(y + dy, ROWS_Y),
            )

    def send_tokens(s, first, last):
        @pl.loop(first, last)
        def _(i):
            p = peer(i)
            remote(tokens.at[:, mine * p + s], qkv.at[s, :, f], token_send, token_recv.at[s], frames=p)

    def send_coloured(s, wanted, first, last):
        end = last if last < shards // 2 else last - lax.rem(colour + wanted + 1, 2)

        @pl.loop(first, end)
        def _(i):
            p = peer_of(shards // 2 - 1 - i, wanted)
            remote(tokens.at[:, mine * p + s], qkv.at[s, :, f], token_send, token_recv.at[s], frames=p)

    def frame_attention(s):
        unit = s * (1 + colour)

        with scope(f"wait_tokens{s}"):
            keep[s].wait()
            await_bytes(qkv.at[s, :, pl.ds(1, shards - 1)], token_recv.at[s])

        def head(h, _):
            hs = pl.ds(pl.multiple_of(h * HEAD_DIM, HEAD_DIM), HEAD_DIM)
            q, k, v = (qkv[s, i, :, :, hs].reshape(shards * here, HEAD_DIM) for i in range(3))
            scores = dot_t(q, k)
            peak = jnp.max(scores, axis=1, keepdims=True)
            p = jnp.exp2((scores - peak) * EXP2_SCALE)
            got = dot(p.astype(jnp.bfloat16), v) / jnp.sum(p, axis=1, keepdims=True)
            o_here[s, :, :, hs] = got.astype(jnp.bfloat16).reshape(shards, here, HEAD_DIM)
            return 0

        with scope(f"frame_attention{s}"):
            lax.fori_loop(0, heads, head, 0)

        @pl.loop(1, shards)
        def _(i):
            p = peer(i)
            remote(o_here.at[s, p], o_back.at[s, f], o_send, o_recv.at[unit], frames=p)

        pltpu.make_async_copy(o_here.at[s, f], o_back.at[s, f], o_recv.at[unit]).start()

    alive = live[1, f] > 0
    keys = levels * ROWS_Y * listed.shape[4]

    def bank_head(h, _):
        hs = pl.ds(pl.multiple_of(h * HEAD_DIM, HEAD_DIM), HEAD_DIM)
        for block in range(2):
            rows = spatial // 2
            q = qv[pl.ds(block * rows, rows), :, hs].reshape(rows * here, HEAD_DIM)
            s0 = dot_t(q, listed[0, 0, :, :, :, hs].reshape(keys, HEAD_DIM))
            s1 = dot_t(q, listed[0, 1, :, :, :, hs].reshape(keys, HEAD_DIM))
            peak1 = jnp.max(s1, axis=1, keepdims=True)
            peak = jnp.max(s0, axis=1, keepdims=True)
            peak = jnp.where(alive, jnp.maximum(peak, peak1), peak)
            p0 = jnp.exp2((s0 - peak) * EXP2_SCALE)
            p1 = jnp.exp2((s1 - jnp.where(alive, peak, FAR)) * EXP2_SCALE)
            total = jnp.sum(p0, axis=1, keepdims=True) + jnp.sum(p1, axis=1, keepdims=True)
            got = dot(p0.astype(jnp.bfloat16), listed[1, 0, :, :, :, hs].reshape(keys, HEAD_DIM))
            got += dot(p1.astype(jnp.bfloat16), listed[1, 1, :, :, :, hs].reshape(keys, HEAD_DIM))
            ref_out[pl.ds(block * rows // mine, rows // mine), :, :, hs] = (got / total).reshape(
                rows // mine, mine, here, HEAD_DIM
            )
        return 0

    order = (lax.rem(x + 2, chips), lax.rem(x + 1, chips), lax.rem(x + chips - 1, chips), x)
    homes = shards // chips
    chunk = weight.shape[1] // CHUNKS
    tile = chunk // 2

    def project(u, between=None):
        s = min(u, 1)
        rows = unit_rows(u, here)
        with scope(f"wait_o{u}"):
            await_bytes(o_back.at[s, pl.ds(0, shards if u == 0 else shards // 2)], o_recv.at[u])
        with scope(f"project{u}"):
            for k, dest in enumerate(order):
                for c in range(2):
                    base = pl.multiple_of(dest * homes, homes) + c * ROWS_Y
                    at = (k * 2 + c) * rows
                    if u == 0:
                        span = pl.ds(base, ROWS_Y)
                        value = ref_out[span, s] + o_back[s, span].astype(jnp.float32)
                        combined[pl.ds(at, rows), :] = value.astype(jnp.bfloat16).reshape(rows, width)
                        continue
                    for j in range(2):
                        p = base + (u - 1 + c) % 2 + 2 * j
                        value = ref_out[p, s] + o_back[s, p].astype(jnp.float32)
                        combined[pl.ds(at + j * here, here), :] = value.astype(jnp.bfloat16)
            for n in range(CHUNKS + LAG):
                if n < CHUNKS:
                    for t in range(2):
                        cs = pl.ds(n * chunk + t * tile, tile)
                        part[u][n, :, :, :, pl.ds(t * tile, tile)] = (
                            dot(combined[pl.ds(0, chips * 2 * rows), :], wv[:, cs])
                            .astype(jnp.bfloat16).reshape(chips, 2, rows, tile)
                        )
                    remote(part[u].at[n, :, 1 - core], pair[u].at[n], pair_send, pair_recv.at[u, n], heads=twin)
                if between is not None and n < CHUNKS:
                    between(n)
                if n >= LAG and u:
                    first_hop(u, n - LAG)

    def both(u, n, k):
        return part[u][n, k, core].astype(jnp.float32) + pair[u][n, k].astype(jnp.float32)

    def first_hop(u, n):
        h2 = unit_rows(u, here) // 2
        await_bytes(pair[u].at[n], pair_recv.at[u, n])
        summed[u][n, 0] = both(u, n, 0).astype(jnp.bfloat16)
        remote(summed[u].at[n, 0, pl.ds(0, h2)], half_l[u].at[n], half_send, half_recv.at[0, u, n], heads=right)
        remote(summed[u].at[n, 0, pl.ds(h2, h2)], half_r[u].at[n], half_send, half_recv.at[1, u, n], heads=left)

    def second_hop(u):
        with scope(f"second_hop{u}"):
            @pl.loop(0, CHUNKS)
            def _(n):
                second_hop_chunk(u, n)

    def second_hop_chunk(u, n):
        h2 = unit_rows(u, here) // 2
        await_bytes(half_l[u].at[n], half_recv.at[0, u, n])
        value = both(u, n, 1)
        top = value[:h2] + half_l[u][n].astype(jnp.float32)
        summed[u][n, 1, pl.ds(0, h2)] = top.astype(jnp.bfloat16)
        summed[u][n, 1, pl.ds(h2, h2)] = value[h2:].astype(jnp.bfloat16)
        remote(summed[u].at[n, 1], full_l[u].at[n], full_send, full_recv.at[0, u, n], heads=right)
        await_bytes(half_r[u].at[n], half_recv.at[1, u, n])
        value = both(u, n, 2)
        low = value[h2:] + half_r[u][n].astype(jnp.float32)
        summed[u][n, 2, pl.ds(0, h2)] = value[:h2].astype(jnp.bfloat16)
        summed[u][n, 2, pl.ds(h2, h2)] = low.astype(jnp.bfloat16)
        remote(summed[u].at[n, 2], full_r[u].at[n], full_send, full_recv.at[1, u, n], heads=left)

    def finish(u):
        with scope(f"finish{u}"):
            @pl.loop(0, CHUNKS)
            def _(n):
                await_bytes(full_l[u].at[n], full_recv.at[0, u, n])
                await_bytes(full_r[u].at[n], full_recv.at[1, u, n])
                value = both(u, n, 3) + full_l[u][n].astype(jnp.float32) + full_r[u][n].astype(jnp.float32)
                value = value.astype(jnp.bfloat16)
                cs = pl.ds(pl.multiple_of(n * chunk, chunk), chunk)
                if u == 0:
                    out[:, 0, :, cs] = value.reshape(ROWS_Y, here, chunk)
                    pltpu.make_async_copy(out.at[:, 0, :, cs], out_hbm.at[:, 0, :, cs], out_sem).start()
                else:
                    for j in range(2):
                        at = lax.rem(u - 1 + core, 2) + 2 * j
                        out[at, 1, :, cs] = value[j * here:(j + 1) * here]
                        pltpu.make_async_copy(out.at[at, 1, :, cs], out_hbm.at[at, 1, :, cs], out_sem).start()

    with scope("own"):
        for kv in range(2):
            pass_on(kv, 0, 1, True)
            pass_on(kv, 0, levels - 1, False)
        send_tokens(0, shards - EARLY + 1, shards)
        for kv in range(2):
            own[kv].wait()
            pick(kv, 0)
    for step in range(1, half + 1):
        if step == half:
            send_tokens(0, 1, shards - EARLY + 1)
            send_coloured(1, 0, 0, AHEAD)
        with scope(f"ring{step}"):
            for kv in range(2):
                for rel, upward in ((step, True), (levels - step, False)):
                    if step == half and upward != (kv == 0):
                        continue
                    await_bytes(held[kv][rel], ring_recv.at[kv, rel])
                    last = half if upward == (kv == 0) else half - 1
                    if step < last:
                        pass_on(kv, rel, rel + 1 if upward else rel - 1, upward)
                    pick(kv, rel)

    frame_attention(0)
    send_coloured(1, 0, AHEAD, shards // 2)
    send_coloured(1, 1, 0, shards // 2)

    with scope("wait_picks"):
        load_q.wait()
        for kv in range(2):
            await_bytes(listed.at[kv, :, :, pl.ds(1, ROWS_Y - 1)], pick_recv.at[kv])
    with scope("bank_attention"):
        lax.fori_loop(0, heads, bank_head, 0)
    load_w.wait()
    project(0)

    with scope("first_hop0"):
        for n in range(CHUNKS):
            first_hop(0, n)

    @pl.when(colour == 0)
    def _():
        frame_attention(1)

    second_hop(0)

    @pl.when(colour == 1)
    def _():
        frame_attention(1)

    project(1)
    finish(0)
    for n in range(START):
        second_hop_chunk(1, n)
    project(2, lambda n: second_hop_chunk(1, n + START) if n + START < CHUNKS else None)
    second_hop(2)
    finish(1)
    finish(2)

    with scope("drain"):
        await_bytes(out, out_sem)
        for kv in range(2):
            for rel in range(1, levels):
                await_bytes(held[kv][rel], ring_send.at[kv, rel])
        await_bytes(picked, pick_send)
        for s in range(mine):
            await_bytes(qkv.at[s, :, pl.ds(1, shards - 1)], token_send)
            await_bytes(o_back.at[s, pl.ds(1, shards - 1)], o_send)
        for u in range(UNITS):
            await_bytes(pair[u], pair_send)
            await_bytes(half_l[u], half_send)
            await_bytes(half_r[u], half_send)
            await_bytes(full_l[u], full_send)
            await_bytes(full_r[u], full_send)


def local(dims, bank_query, char_bank, char_slots, slot_live, frame_tokens, out_weight):
    shards, levels, chips = dims
    spatial, here, width = bank_query.shape
    _, characters, ref_here, _ = char_bank.shape
    mine = spatial // shards
    columns = out_weight.shape[1]
    homes = shards // chips
    chunk = columns // CHUNKS
    rows = [unit_rows(u, here) for u in range(UNITS)]
    bf16, f32 = jnp.bfloat16, jnp.float32
    dma = pltpu.SemaphoreType.DMA
    vmem = pltpu.VMEM
    scratch = [vmem((characters, ref_here, width), bf16) for _ in range(2 * levels)] + [
        vmem((2, levels, ROWS_Y - 1, 2, ref_here, width), bf16),
        vmem((2, 2, levels, ROWS_Y, ref_here, width), bf16),
        vmem((spatial, here, width), bf16),
        vmem((width, columns), bf16),
        vmem((mine, 3, shards, here, width), bf16),
        vmem((mine, shards, here, width), bf16),
        vmem((mine, shards, here, width), bf16),
        vmem((shards, mine, here, width), f32),
        vmem((shards * here, width), bf16),
        vmem((homes // 2, mine, here, columns), bf16),
        *[vmem((CHUNKS, chips, 2, n, chunk), bf16) for n in rows],
        *[vmem((CHUNKS, chips, n, chunk), bf16) for n in rows],
        *[vmem((CHUNKS, 3, n, chunk), bf16) for n in rows],
        *[vmem((CHUNKS, n // 2, chunk), bf16) for n in rows * 2],
        *[vmem((CHUNKS, n, chunk), bf16) for n in rows * 2],
        dma((4,)), dma((2, levels)), dma((2, levels)), dma(()), dma((2,)), dma(()), dma((mine,)), dma(()), dma((UNITS,)),
        dma(()), dma((UNITS, CHUNKS)), dma(()), dma((2, UNITS, CHUNKS)), dma(()), dma((2, UNITS, CHUNKS)), dma((1, mine)), dma(()),
    ]
    smem = pl.BlockSpec(memory_space=pltpu.SMEM)
    anywhere = pl.BlockSpec(memory_space=pl.ANY)
    out = pl.pallas_call(
        functools.partial(kernel, dims),
        out_shape=jax.ShapeDtypeStruct((homes // 2, mine, here, columns), bf16),
        in_specs=[smem, smem, anywhere, anywhere, anywhere, anywhere],
        out_specs=anywhere,
        scratch_shapes=scratch,
        compiler_params=pltpu.CompilerParams(
            collective_id=0, has_side_effects=True, vmem_limit_bytes=60 * 1024 * 1024
        ),
        name="block",
    )(char_slots.T, slot_live.T, bank_query, char_bank, frame_tokens, out_weight)
    return out.reshape(homes // 2 * mine, here, columns)


def solution(mesh):
    shards = mesh.shape["frames"]
    dims = (shards, shards // ROWS_Y, mesh.shape["heads"] // 2)
    in_specs = (
        P(None, "frames", "heads"),
        P(None, None, "frames", "heads"),
        P(),
        P(),
        P(None, None, "frames", "heads"),
        P("heads", None),
    )
    return jax.shard_map(
        functools.partial(local, dims), mesh=mesh, in_specs=in_specs, out_specs=P("heads", "frames", None), check_vma=False
    )
```

```python
import functools

import jax
import jax.numpy as jnp
from jax import lax
from jax.experimental import pallas as pl
from jax.experimental.pallas import tpu as pltpu
from jax.sharding import PartitionSpec as P

HEAD_DIM = 128
ROWS_Y = 4
CHUNKS = 4
UNITS = 3
EARLY = 4
AHEAD = 6
LAG = 2
EXP2_SCALE = HEAD_DIM ** -0.5 * 1.4426950408889634
FAR = 1e30
MESH = pl.DeviceIdType.MESH
scope = jax.named_scope


def dot_t(a, b):
    return lax.dot_general(a, b, (((1,), (1,)), ((), ())), preferred_element_type=jnp.float32)


def dot(a, b):
    return jnp.dot(a, b, preferred_element_type=jnp.float32)


def await_bytes(ref, sem):
    pltpu.make_async_copy(ref, ref, sem).wait()


def remote(src, dst, send, recv, **where):
    pltpu.make_async_remote_copy(
        src_ref=src, dst_ref=dst, send_sem=send, recv_sem=recv, device_id=where, device_id_type=MESH
    ).start()


def unit_rows(u, here):
    return here * (ROWS_Y if u == 0 else ROWS_Y // 2)


def kernel(dims, slots, live, queries, bank, tokens, weight, out_hbm, *scratch):
    shards, levels, chips = dims
    held = (scratch[0:levels], scratch[levels:2 * levels])
    (picked, listed, qv, wv, qkv, o_here, o_back, ref_out, combined, out) = scratch[2 * levels:2 * levels + 10]
    buffers = scratch[2 * levels + 10:-17]
    part, pair, summed, half_l, half_r, full_l, full_r = (buffers[i * UNITS:(i + 1) * UNITS] for i in range(7))
    (local_sem, ring_send, ring_recv, pick_send, pick_recv, token_send, token_recv, o_send, o_recv, pair_send, pair_recv,
     half_send, half_recv, full_send, full_recv, own_sem, out_sem) = scratch[-17:]
    spatial, here, width = queries.shape
    heads = width // HEAD_DIM
    mine = spatial // shards
    half = levels // 2
    f = lax.axis_index("frames")
    r = lax.axis_index("heads")
    z, y = lax.div(f, ROWS_Y), lax.rem(f, ROWS_Y)
    x, core = lax.div(r, 2), lax.rem(r, 2)
    up = lax.rem(z + 1, levels) * ROWS_Y + y
    down = lax.rem(z + levels - 1, levels) * ROWS_Y + y
    twin = r + 1 - 2 * core
    right = lax.rem(x + 1, chips) * 2 + core
    left = lax.rem(x + chips - 1, chips) * 2 + core

    colour = lax.rem(z + y, 2)

    def place(k, dy):
        odd = lax.rem(k, 2)
        dz = odd * lax.div(k + 1, 2) + (1 - odd) * (levels - lax.div(k, 2))
        return lax.rem(z + dz, levels), lax.rem(y + dy, ROWS_Y)

    def peer(i):
        i = shards - i
        there_z, there_y = place(lax.div(i, ROWS_Y), lax.rem(i, ROWS_Y))
        return there_z * ROWS_Y + there_y

    def peer_of(i, wanted):
        there_z, _ = place(lax.div(i, 2), 0)
        dy = lax.rem(there_z + y + wanted, 2) + 2 * lax.rem(i, 2)
        return there_z * ROWS_Y + lax.rem(y + dy, ROWS_Y)

    own = [pltpu.make_async_copy(bank.at[kv], held[kv][0], local_sem.at[kv]) for kv in range(2)]
    load_q = pltpu.make_async_copy(queries, qv, local_sem.at[2])
    load_w = pltpu.make_async_copy(weight, wv, local_sem.at[3])
    keep = [pltpu.make_async_copy(tokens.at[:, mine * f + s], qkv.at[s, :, f], own_sem.at[0, s]) for s in range(mine)]
    for copy in (*own, load_q, *keep, load_w):
        copy.start()

    with scope("barrier"):
        barrier = pltpu.get_barrier_semaphore()

        @pl.loop(1, shards)
        def _(i):
            pl.semaphore_signal(barrier, inc=1, device_id={"frames": peer(i)}, device_id_type=MESH)

        for near in (twin, right, left):
            pl.semaphore_signal(barrier, inc=1, device_id={"heads": near}, device_id_type=MESH)
        pl.semaphore_wait(barrier, shards - 1 + 3)

    def pass_on(kv, src, rel, upward):
        ref = bank.at[kv] if src == 0 else held[kv][src]
        remote(ref, held[kv][rel], ring_send.at[kv, rel], ring_recv.at[kv, rel], frames=up if upward else down)

    def pick(kv, rel):
        for dy in range(ROWS_Y):
            shard = z * ROWS_Y + lax.rem(y + dy, ROWS_Y)
            for j in range(2):
                block = held[kv][rel][slots[j, shard]]
                if dy:
                    picked[kv, rel, dy - 1, j] = block
                else:
                    listed[kv, j, rel, 0] = block
        for dy in range(1, ROWS_Y):
            remote(
                picked.at[kv, rel, dy - 1], listed.at[kv, :, rel, dy], pick_send, pick_recv.at[kv],
                frames=z * ROWS_Y + lax.rem(y + dy, ROWS_Y),
            )

    def send_tokens(s, first, last):
        @pl.loop(first, last)
        def _(i):
            p = peer(i)
            remote(tokens.at[:, mine * p + s], qkv.at[s, :, f], token_send, token_recv.at[s], frames=p)

    def send_coloured(s, wanted, first, last):
        end = last if last < shards // 2 else last - lax.rem(colour + wanted + 1, 2)

        @pl.loop(first, end)
        def _(i):
            p = peer_of(shards // 2 - 1 - i, wanted)
            remote(tokens.at[:, mine * p + s], qkv.at[s, :, f], token_send, token_recv.at[s], frames=p)

    def frame_attention(s):
        unit = s * (1 + colour)

        with scope(f"wait_tokens{s}"):
            keep[s].wait()
            await_bytes(qkv.at[s, :, pl.ds(1, shards - 1)], token_recv.at[s])

        def head(h, _):
            hs = pl.ds(pl.multiple_of(h * HEAD_DIM, HEAD_DIM), HEAD_DIM)
            q, k, v = (qkv[s, i, :, :, hs].reshape(shards * here, HEAD_DIM) for i in range(3))
            scores = dot_t(q, k)
            peak = jnp.max(scores, axis=1, keepdims=True)
            p = jnp.exp2((scores - peak) * EXP2_SCALE)
            got = dot(p.astype(jnp.bfloat16), v) / jnp.sum(p, axis=1, keepdims=True)
            o_here[s, :, :, hs] = got.astype(jnp.bfloat16).reshape(shards, here, HEAD_DIM)
            return 0

        with scope(f"frame_attention{s}"):
            lax.fori_loop(0, heads, head, 0, unroll=True)

        @pl.loop(1, shards)
        def _(i):
            p = peer(i)
            remote(o_here.at[s, p], o_back.at[s, f], o_send, o_recv.at[unit], frames=p)

        pltpu.make_async_copy(o_here.at[s, f], o_back.at[s, f], o_recv.at[unit]).start()

    alive = live[1, f] > 0
    keys = levels * ROWS_Y * listed.shape[4]

    def bank_head(h, _):
        hs = pl.ds(pl.multiple_of(h * HEAD_DIM, HEAD_DIM), HEAD_DIM)
        for block in range(2):
            rows = spatial // 2
            q = qv[pl.ds(block * rows, rows), :, hs].reshape(rows * here, HEAD_DIM)
            s0 = dot_t(q, listed[0, 0, :, :, :, hs].reshape(keys, HEAD_DIM))
            s1 = dot_t(q, listed[0, 1, :, :, :, hs].reshape(keys, HEAD_DIM))
            peak1 = jnp.max(s1, axis=1, keepdims=True)
            peak = jnp.max(s0, axis=1, keepdims=True)
            peak = jnp.where(alive, jnp.maximum(peak, peak1), peak)
            p0 = jnp.exp2((s0 - peak) * EXP2_SCALE)
            p1 = jnp.exp2((s1 - jnp.where(alive, peak, FAR)) * EXP2_SCALE)
            total = jnp.sum(p0, axis=1, keepdims=True) + jnp.sum(p1, axis=1, keepdims=True)
            got = dot(p0.astype(jnp.bfloat16), listed[1, 0, :, :, :, hs].reshape(keys, HEAD_DIM))
            got += dot(p1.astype(jnp.bfloat16), listed[1, 1, :, :, :, hs].reshape(keys, HEAD_DIM))
            ref_out[pl.ds(block * rows // mine, rows // mine), :, :, hs] = (got / total).reshape(
                rows // mine, mine, here, HEAD_DIM
            )
        return 0

    order = (lax.rem(x + 2, chips), lax.rem(x + 1, chips), lax.rem(x + chips - 1, chips), x)
    homes = shards // chips
    chunk = weight.shape[1] // CHUNKS
    tile = chunk // 2

    def project(u, between=None):
        s = min(u, 1)
        rows = unit_rows(u, here)
        with scope(f"wait_o{u}"):
            await_bytes(o_back.at[s, pl.ds(0, shards if u == 0 else shards // 2)], o_recv.at[u])
        with scope(f"project{u}"):
            for k, dest in enumerate(order):
                for c in range(2):
                    base = pl.multiple_of(dest * homes, homes) + c * ROWS_Y
                    at = (k * 2 + c) * rows
                    if u == 0:
                        span = pl.ds(base, ROWS_Y)
                        value = ref_out[span, s] + o_back[s, span].astype(jnp.float32)
                        combined[pl.ds(at, rows), :] = value.astype(jnp.bfloat16).reshape(rows, width)
                        continue
                    for j in range(2):
                        p = base + (u - 1 + c) % 2 + 2 * j
                        value = ref_out[p, s] + o_back[s, p].astype(jnp.float32)
                        combined[pl.ds(at + j * here, here), :] = value.astype(jnp.bfloat16)
            for n in range(CHUNKS + LAG):
                if n < CHUNKS:
                    for t in range(2):
                        cs = pl.ds(n * chunk + t * tile, tile)
                        part[u][n, :, :, :, pl.ds(t * tile, tile)] = (
                            dot(combined[pl.ds(0, chips * 2 * rows), :], wv[:, cs])
                            .astype(jnp.bfloat16).reshape(chips, 2, rows, tile)
                        )
                    remote(part[u].at[n, :, 1 - core], pair[u].at[n], pair_send, pair_recv.at[u, n], heads=twin)
                if between is not None and n < CHUNKS:
                    between(n)
                if n >= LAG and u:
                    first_hop(u, n - LAG)

    def both(u, n, k):
        return part[u][n, k, core].astype(jnp.float32) + pair[u][n, k].astype(jnp.float32)

    def first_hop(u, n):
        h2 = unit_rows(u, here) // 2
        await_bytes(pair[u].at[n], pair_recv.at[u, n])
        summed[u][n, 0] = both(u, n, 0).astype(jnp.bfloat16)
        remote(summed[u].at[n, 0, pl.ds(0, h2)], half_l[u].at[n], half_send, half_recv.at[0, u, n], heads=right)
        remote(summed[u].at[n, 0, pl.ds(h2, h2)], half_r[u].at[n], half_send, half_recv.at[1, u, n], heads=left)

    def second_hop(u):
        with scope(f"second_hop{u}"):
            @pl.loop(0, CHUNKS)
            def _(n):
                second_hop_chunk(u, n)

    def second_hop_chunk(u, n):
        h2 = unit_rows(u, here) // 2
        await_bytes(half_l[u].at[n], half_recv.at[0, u, n])
        value = both(u, n, 1)
        top = value[:h2] + half_l[u][n].astype(jnp.float32)
        summed[u][n, 1, pl.ds(0, h2)] = top.astype(jnp.bfloat16)
        summed[u][n, 1, pl.ds(h2, h2)] = value[h2:].astype(jnp.bfloat16)
        remote(summed[u].at[n, 1], full_l[u].at[n], full_send, full_recv.at[0, u, n], heads=right)
        await_bytes(half_r[u].at[n], half_recv.at[1, u, n])
        value = both(u, n, 2)
        low = value[h2:] + half_r[u][n].astype(jnp.float32)
        summed[u][n, 2, pl.ds(0, h2)] = value[:h2].astype(jnp.bfloat16)
        summed[u][n, 2, pl.ds(h2, h2)] = low.astype(jnp.bfloat16)
        remote(summed[u].at[n, 2], full_r[u].at[n], full_send, full_recv.at[1, u, n], heads=left)

    def finish(u):
        with scope(f"finish{u}"):
            @pl.loop(0, CHUNKS)
            def _(n):
                await_bytes(full_l[u].at[n], full_recv.at[0, u, n])
                await_bytes(full_r[u].at[n], full_recv.at[1, u, n])
                value = both(u, n, 3) + full_l[u][n].astype(jnp.float32) + full_r[u][n].astype(jnp.float32)
                value = value.astype(jnp.bfloat16)
                cs = pl.ds(pl.multiple_of(n * chunk, chunk), chunk)
                if u == 0:
                    out[:, 0, :, cs] = value.reshape(ROWS_Y, here, chunk)
                    pltpu.make_async_copy(out.at[:, 0, :, cs], out_hbm.at[:, 0, :, cs], out_sem).start()
                else:
                    for j in range(2):
                        at = lax.rem(u - 1 + core, 2) + 2 * j
                        out[at, 1, :, cs] = value[j * here:(j + 1) * here]
                        pltpu.make_async_copy(out.at[at, 1, :, cs], out_hbm.at[at, 1, :, cs], out_sem).start()

    with scope("own"):
        for kv in range(2):
            pass_on(kv, 0, 1, True)
            pass_on(kv, 0, levels - 1, False)
        send_tokens(0, shards - EARLY + 1, shards)
        for kv in range(2):
            own[kv].wait()
            pick(kv, 0)
    for step in range(1, half + 1):
        if step == half:
            send_tokens(0, 1, shards - EARLY + 1)
            send_coloured(1, 0, 0, AHEAD)
        with scope(f"ring{step}"):
            for kv in range(2):
                for rel, upward in ((step, True), (levels - step, False)):
                    if step == half and upward != (kv == 0):
                        continue
                    await_bytes(held[kv][rel], ring_recv.at[kv, rel])
                    last = half if upward == (kv == 0) else half - 1
                    if step < last:
                        pass_on(kv, rel, rel + 1 if upward else rel - 1, upward)
                    pick(kv, rel)

    frame_attention(0)

    def send_rest():
        send_coloured(1, 0, AHEAD, shards // 2)
        send_coloured(1, 1, 0, shards // 2)

    pl.when(core == 1)(send_rest)

    with scope("wait_picks"):
        load_q.wait()
        for kv in range(2):
            await_bytes(listed.at[kv, :, :, pl.ds(1, ROWS_Y - 1)], pick_recv.at[kv])
    with scope("bank_attention"):
        lax.fori_loop(0, heads, bank_head, 0)
    pl.when(core == 0)(send_rest)
    load_w.wait()
    project(0)

    with scope("first_hop0"):
        for n in range(CHUNKS):
            first_hop(0, n)

    @pl.when(colour == 0)
    def _():
        frame_attention(1)

    second_hop(0)

    @pl.when(colour == 1)
    def _():
        frame_attention(1)

    project(1)
    finish(0)

    def second_hops(n):
        for m in ((), (0, 1), (2,), (3,))[n]:
            second_hop_chunk(1, m)

    project(2, second_hops)
    second_hop(2)
    finish(1)
    finish(2)

    with scope("drain"):
        await_bytes(out, out_sem)
        for kv in range(2):
            for rel in range(1, levels):
                await_bytes(held[kv][rel], ring_send.at[kv, rel])
        await_bytes(picked, pick_send)
        for s in range(mine):
            await_bytes(qkv.at[s, :, pl.ds(1, shards - 1)], token_send)
            await_bytes(o_back.at[s, pl.ds(1, shards - 1)], o_send)
        for u in range(UNITS):
            await_bytes(pair[u], pair_send)
            await_bytes(half_l[u], half_send)
            await_bytes(half_r[u], half_send)
            await_bytes(full_l[u], full_send)
            await_bytes(full_r[u], full_send)


def local(dims, bank_query, char_bank, char_slots, slot_live, frame_tokens, out_weight):
    shards, levels, chips = dims
    spatial, here, width = bank_query.shape
    _, characters, ref_here, _ = char_bank.shape
    mine = spatial // shards
    columns = out_weight.shape[1]
    homes = shards // chips
    chunk = columns // CHUNKS
    rows = [unit_rows(u, here) for u in range(UNITS)]
    bf16, f32 = jnp.bfloat16, jnp.float32
    dma = pltpu.SemaphoreType.DMA
    vmem = pltpu.VMEM
    scratch = [vmem((characters, ref_here, width), bf16) for _ in range(2 * levels)] + [
        vmem((2, levels, ROWS_Y - 1, 2, ref_here, width), bf16),
        vmem((2, 2, levels, ROWS_Y, ref_here, width), bf16),
        vmem((spatial, here, width), bf16),
        vmem((width, columns), bf16),
        vmem((mine, 3, shards, here, width), bf16),
        vmem((mine, shards, here, width), bf16),
        vmem((mine, shards, here, width), bf16),
        vmem((shards, mine, here, width), f32),
        vmem((shards * here, width), bf16),
        vmem((homes // 2, mine, here, columns), bf16),
        *[vmem((CHUNKS, chips, 2, n, chunk), bf16) for n in rows],
        *[vmem((CHUNKS, chips, n, chunk), bf16) for n in rows],
        *[vmem((CHUNKS, 3, n, chunk), bf16) for n in rows],
        *[vmem((CHUNKS, n // 2, chunk), bf16) for n in rows * 2],
        *[vmem((CHUNKS, n, chunk), bf16) for n in rows * 2],
        dma((4,)), dma((2, levels)), dma((2, levels)), dma(()), dma((2,)), dma(()), dma((mine,)), dma(()), dma((UNITS,)),
        dma(()), dma((UNITS, CHUNKS)), dma(()), dma((2, UNITS, CHUNKS)), dma(()), dma((2, UNITS, CHUNKS)), dma((1, mine)), dma(()),
    ]
    smem = pl.BlockSpec(memory_space=pltpu.SMEM)
    anywhere = pl.BlockSpec(memory_space=pl.ANY)
    out = pl.pallas_call(
        functools.partial(kernel, dims),
        out_shape=jax.ShapeDtypeStruct((homes // 2, mine, here, columns), bf16),
        in_specs=[smem, smem, anywhere, anywhere, anywhere, anywhere],
        out_specs=anywhere,
        scratch_shapes=scratch,
        compiler_params=pltpu.CompilerParams(
            collective_id=0, has_side_effects=True, vmem_limit_bytes=60 * 1024 * 1024
        ),
        name="block",
    )(char_slots.T, slot_live.T, bank_query, char_bank, frame_tokens, out_weight)
    return out.reshape(homes // 2 * mine, here, columns)


def solution(mesh):
    shards = mesh.shape["frames"]
    dims = (shards, shards // ROWS_Y, mesh.shape["heads"] // 2)
    in_specs = (
        P(None, "frames", "heads"),
        P(None, None, "frames", "heads"),
        P(),
        P(),
        P(None, None, "frames", "heads"),
        P("heads", None),
    )
    return jax.shard_map(
        functools.partial(local, dims), mesh=mesh, in_specs=in_specs, out_specs=P("heads", "frames", None), check_vma=False
    )
```
